32 devices in a mesh: pb: 16 (over z, y, core), ka: 2 (over x).
Axes of the slice: x: 2, y: 2, z: 4, core: 2. Of those that a mesh axis runs over, the one named last changes fastest.
Arguments:
- queries: bfloat16 [4096, 1024], P('pb')
- keys: bfloat16 [4096, 128], P(('pb', 'ka'))
- values: bfloat16 [4096, 128], P(('pb', 'ka')), may hold values from -6 to 6
- doc_ids: int32 [4096], replicated, may hold values from 0 to 3, as said below
- visible_end: int32 [4096], P('pb'), may hold values from 1 to 4096, as said below
Outputs:
- attended: bfloat16 [4096, 1024], P('pb')
The draws below stay inside these ranges and needn't reach their ends.
Inputs may be any that keep to these rules, and one draw needn't show every extreme that they name: `doc_ids`: non-decreasing along the sequence; the first token is in document 0 and the last in document 4 - 1. visible_end[i] is i + 1 for a text token and the end of its image block for a token inside an image block; some block ends at 4096.
All inputs are finite; a program needn't handle non-finite values.
Results may differ from the reference program's by a relative error of at most 0.014.
Values may be sent and summed in bfloat16 or wider, within the bound.
A program may use at most 192 MiB of HBM per device.

```python
import jax
import jax.numpy as jnp
from jax import lax

HQ = 8
HD = 128
NDOCS = 4
NIMG = 16
SEQ = 4096
IMG_MAX = 256


def key_field(key):
    base = jax.random.normal(jax.random.fold_in(key, 11), (SEQ, HD), jnp.float32)
    return base


def draw_keys(key, part):
    return key_field(key).astype(jnp.bfloat16)


def draw_queries(key, part):
    field = jax.random.normal(jax.random.fold_in(key, 12), (SEQ, HQ, HD), jnp.float32)
    return field.reshape(SEQ, HQ * HD).astype(jnp.bfloat16)


def layout(key):
    index = jnp.arange(SEQ, dtype=jnp.int32)
    cuts = jax.random.randint(jax.random.fold_in(key, 21), (NDOCS - 1,), 1, SEQ)
    documents = jnp.sum((index[:, None] >= cuts[None, :]).astype(jnp.int32), axis=1).astype(jnp.int32)
    starts = jax.random.randint(jax.random.fold_in(key, 22), (NIMG - 1,), 0, SEQ - IMG_MAX)
    spans = jax.random.randint(jax.random.fold_in(key, 23), (NIMG - 1,), IMG_MAX // 4, IMG_MAX + 1)
    starts = jnp.concatenate([jnp.array([SEQ - IMG_MAX], jnp.int32), starts.astype(jnp.int32)])
    ends = jnp.concatenate([jnp.array([SEQ], jnp.int32), jnp.minimum(starts[1:] + spans.astype(jnp.int32), SEQ)])
    inside = (index[None, :] >= starts[:, None]) & (index[None, :] < ends[:, None])
    reach = jnp.max(jnp.where(inside, ends[:, None], 0), axis=0)
    visible = jnp.maximum(index + 1, reach).astype(jnp.int32)
    return (documents, visible)


def draw_doc_ids(key, part):
    return layout(key)[0]


def draw_visible_end(key, part):
    return layout(key)[1]


def level_of(stream_key, extent, split, low, largest):
    factor_of = 1.0
    for axis_at, blocks in split:
        steps = jax.random.uniform(jax.random.fold_in(jax.random.fold_in(stream_key, 6), axis_at), (blocks,), jnp.float32, low / len(split), largest / len(split))
        factor_of = factor_of * jnp.repeat(jnp.exp(steps), extent[axis_at] // blocks).reshape((-1,) + (1,) * (len(extent) - 1 - axis_at))
    return factor_of


def normal_values(own_key, extent, spread, most, split=(), held_as=jnp.bfloat16):
    values = spread * jax.random.normal(own_key, extent, jnp.float32)
    if split:
        values = values * level_of(own_key, extent, split, -0.22, 0.18)
    return jnp.clip(values, -most, most).astype(held_as)


def setup_inputs(seed: int = 0) -> dict:
    arg_keys = jax.random.split(jax.random.key(seed), 6)
    return {
        "queries": draw_queries(jax.random.fold_in(arg_keys[5], 71), 0),
        "keys": draw_keys(jax.random.fold_in(arg_keys[5], 71), 0),
        "values": normal_values(arg_keys[2], (SEQ, HD), 1.0, 6.0, ((0, 32),)),
        "doc_ids": draw_doc_ids(jax.random.fold_in(arg_keys[5], 71), 0),
        "visible_end": draw_visible_end(jax.random.fold_in(arg_keys[5], 71), 0),
    }


def reference(queries, keys, values, doc_ids, visible_end):
    row_block = min(256, SEQ)
    positions = jnp.arange(SEQ, dtype=jnp.int32)
    key_float = keys.astype(jnp.float32)
    value_float = values.astype(jnp.float32)
    scale = 1.0 / (HD ** 0.5)

    def block(start):
        query = lax.dynamic_slice_in_dim(queries, start, row_block, 0).astype(jnp.float32)
        query = query.reshape(row_block, HQ, HD)
        query_doc = lax.dynamic_slice_in_dim(doc_ids, start, row_block, 0)
        query_end = lax.dynamic_slice_in_dim(visible_end, start, row_block, 0)
        scores = jnp.einsum("qhd,kd->hqk", query, key_float) * scale
        allowed = (query_doc[:, None] == doc_ids[None, :]) & (positions[None, :] < query_end[:, None])
        masked = jnp.where(allowed[None], scores, jnp.float32(-1e30))
        rowmax = jnp.max(masked, axis=-1, keepdims=True)
        weights = jnp.where(allowed[None], jnp.exp(masked - rowmax), jnp.float32(0.0))
        total = jnp.sum(weights, axis=-1)
        rounded = lax.optimization_barrier(weights.astype(jnp.bfloat16))
        summed = jnp.einsum("hqk,kd->qhd", rounded.astype(jnp.float32), value_float)
        result = summed / jnp.transpose(total)[:, :, None]
        return result.reshape(row_block, HQ * HD).astype(jnp.bfloat16)

    starts = jnp.arange(0, SEQ, row_block, dtype=jnp.int32)
    blocks = lax.map(block, starts)
    return blocks.reshape(SEQ, HQ * HD)
```

```python
import functools

import jax
import jax.numpy as jnp
from jax import lax
from jax.experimental import pallas as pl
from jax.experimental.pallas import tpu as pltpu
from jax.sharding import PartitionSpec as P

HD = 128
NDOCS = 4
KB = 512
LANES = 128
NEG = -1e30
SCALE = 1.4426950408889634 / HD**0.5
MESH = pl.DeviceIdType.MESH


def gather_kernel(zs, k_ref, v_ref, out, col_s, col_r, x_s, x_r, y_s, y_r, fx_s, fx_r, fy_s, fy_r, c_s, c_r):
    p = lax.axis_index("pb")
    a = lax.axis_index("ka")
    n = k_ref.shape[0]
    z = p // 4
    r = p % 4
    y = r // 2
    c = r % 2
    row_y = z * 4 + (1 - y) * 2 + c
    core_p = z * 4 + y * 2 + (1 - c)
    x_peer = (p, 1 - a)
    y_peer = (row_y, a)
    core_peer = (core_p, a)

    def rows(src_z, ry, cc, aa):
        base = ((src_z * 4 + ry * 2 + cc) * 2 + aa) * n
        return pl.ds(pl.multiple_of(base, n), n)

    mine = rows(z, y, c, a)
    out[0, mine, :] = k_ref[...]
    out[1, mine, :] = v_ref[...]

    barrier = pltpu.get_barrier_semaphore()
    for peer in (x_peer, y_peer, core_peer):
        pl.semaphore_signal(barrier, inc=1, device_id=peer, device_id_type=MESH)
    for d in range(1, zs):
        pl.semaphore_signal(
            barrier, inc=1, device_id=(((z + d) % zs) * 4 + r, a), device_id_type=MESH
        )
    pl.semaphore_wait(barrier, 3 + zs - 1)

    def copy(view, ss, rs, peer):
        return pltpu.make_async_remote_copy(
            src_ref=view, dst_ref=view, send_sem=ss, recv_sem=rs, device_id=peer, device_id_type=MESH
        )

    def both(src_z, ry, cc, aa):
        return out.at[:, rows(src_z, ry, cc, aa), :]

    def one(kv, src_z, ry, cc, aa):
        return out.at[kv, rows(src_z, ry, cc, aa), :]

    order = []
    for step in range(1, zs // 2 + 1):
        for d in (step, zs - step):
            if 0 < d < zs and d not in order:
                order.append(d)
    sends = []

    def go(cp):
        cp.start()
        sends.append(cp)

    for d in order:
        go(copy(both(z, y, c, a), col_s.at[d], col_r.at[d], (((z + d) % zs) * 4 + r, a)))

    def spread(d):
        j = (z - d + zs) % zs
        go(copy(both(j, y, c, a), x_s.at[d], x_r.at[d], x_peer))
        go(copy(both(j, y, c, a), y_s.at[d], y_r.at[d], y_peer))
        go(copy(both(j, y, c, a), c_s.at[0, d], c_r.at[0, d], core_peer))

    def relay(d):
        j = (z - d + zs) % zs
        copy(both(j, y, c, 1 - a), x_s.at[d], x_r.at[d], x_peer).wait_recv()
        go(copy(one(0, j, y, c, 1 - a), fy_s.at[d], fy_r.at[d], y_peer))
        go(copy(both(j, y, c, 1 - a), c_s.at[1, d], c_r.at[1, d], core_peer))
        copy(both(j, 1 - y, c, a), y_s.at[d], y_r.at[d], y_peer).wait_recv()
        go(copy(one(1, j, 1 - y, c, a), fx_s.at[d], fx_r.at[d], x_peer))
        go(copy(both(j, 1 - y, c, a), c_s.at[2, d], c_r.at[2, d], core_peer))

    def last(d):
        j = (z - d + zs) % zs
        copy(one(0, j, 1 - y, c, 1 - a), fy_s.at[d], fy_r.at[d], y_peer).wait_recv()
        go(copy(one(0, j, 1 - y, c, 1 - a), c_s.at[3, d], c_r.at[3, d], core_peer))
        copy(one(1, j, 1 - y, c, 1 - a), fx_s.at[d], fx_r.at[d], x_peer).wait_recv()
        go(copy(one(1, j, 1 - y, c, 1 - a), c_s.at[4, d], c_r.at[4, d], core_peer))

    seq = [0] + order
    for i in range(zs + 2):
        if i < zs:
            d = seq[i]
            if d > 0:
                j = (z - d + zs) % zs
                copy(both(j, y, c, a), col_s.at[d], col_r.at[d], x_peer).wait_recv()
            spread(d)
        if 1 <= i < zs + 1:
            relay(seq[i - 1])
        if i >= 2:
            last(seq[i - 2])
    for d in seq:
        j = (z - d + zs) % zs
        copy(both(j, y, 1 - c, a), c_s.at[0, d], c_r.at[0, d], core_peer).wait_recv()
        copy(both(j, y, 1 - c, 1 - a), c_s.at[1, d], c_r.at[1, d], core_peer).wait_recv()
        copy(both(j, 1 - y, 1 - c, a), c_s.at[2, d], c_r.at[2, d], core_peer).wait_recv()
        copy(one(0, j, 1 - y, 1 - c, 1 - a), c_s.at[3, d], c_r.at[3, d], core_peer).wait_recv()
        copy(one(1, j, 1 - y, 1 - c, 1 - a), c_s.at[4, d], c_r.at[4, d], core_peer).wait_recv()
    for cp in sends:
        cp.wait_send()


def gather(keys, values, shards):
    zs = shards // 4
    n = keys.shape[0]
    dma = pltpu.SemaphoreType.DMA
    return pl.pallas_call(
        functools.partial(gather_kernel, zs),
        out_shape=jax.ShapeDtypeStruct((2, n * shards * 2, HD), jnp.bfloat16),
        in_specs=[pl.BlockSpec(memory_space=pltpu.VMEM)] * 2,
        out_specs=pl.BlockSpec(memory_space=pltpu.VMEM),
        scratch_shapes=[dma((zs,))] * 10 + [dma((5, zs))] * 2,
        compiler_params=pltpu.CompilerParams(
            collective_id=0, has_side_effects=True, vmem_limit_bytes=40 * 2**20
        ),
        name="gather_kv",
    )(keys, values)


def attend_kernel(q_ref, kv_ref, doc_ref, end_ref, o_ref, s_ref, vx_ref, acc_ref, mx_ref, lo_ref, hi_ref):
    rows = q_ref.shape[0]
    heads = q_ref.shape[1] // HD
    seq = kv_ref.shape[1]
    pos0 = lax.axis_index("pb") * rows
    docs = doc_ref[...]
    starts = [jnp.sum((docs < d).astype(jnp.int32)) for d in range(1, NDOCS)]
    pos = pos0 + lax.broadcasted_iota(jnp.int32, (1, rows), 1)
    lo = jnp.zeros((1, rows), jnp.int32)
    hi = jnp.minimum(end_ref[...], seq)
    for s in starts:
        lo = jnp.maximum(lo, jnp.where(pos >= s, s, 0))
        hi = jnp.minimum(hi, jnp.where(pos < s, s, seq))
    for t in range(rows // LANES):
        cut = slice(t * LANES, (t + 1) * LANES)
        lo_ref[cut, :] = jnp.transpose(jnp.broadcast_to(lo[:, cut], (LANES, LANES)))
        hi_ref[cut, :] = jnp.transpose(jnp.broadcast_to(hi[:, cut], (LANES, LANES)))
    lo_min = jnp.min(lo)
    lo_max = jnp.max(lo)
    hi_min = jnp.min(hi)
    hi_max = jnp.max(hi)
    first = (lo_min // LANES) * LANES
    blocks = (hi_max - first + KB - 1) // KB
    first = jnp.minimum(first, seq - blocks * KB)

    def start_of(k):
        return pl.multiple_of(first + k * KB, LANES)

    lanes = lax.broadcasted_iota(jnp.int32, (rows, LANES), 1)

    def fill(k, _):
        at = start_of(k)
        vx_ref[pl.ds(at, KB), 0:HD] = kv_ref[1, pl.ds(at, KB), :]
        vx_ref[pl.ds(at, KB), HD : 2 * HD] = jnp.ones((KB, HD), jnp.bfloat16)
        return 0

    lax.fori_loop(0, blocks, fill, 0)

    def score(h, k, masked):
        at = start_of(k)
        slot = h % 2
        s = lax.dot_general(
            q_ref[:, h * HD : (h + 1) * HD],
            kv_ref[0, pl.ds(at, KB), :],
            (((1,), (1,)), ((), ())),
            preferred_element_type=jnp.float32,
        )
        top = mx_ref[slot]
        if masked:
            lo_at = lo_ref[...] - at
            hi_at = hi_ref[...] - at
        for t in range(KB // LANES):
            part = s[:, t * LANES : (t + 1) * LANES]
            if masked:
                where = lanes + t * LANES
                part = jnp.where((where >= lo_at) & (where < hi_at), part, NEG)
            s_ref[slot, k, :, t * LANES : (t + 1) * LANES] = part
            top = jnp.maximum(top, part)
        mx_ref[slot] = top

    def weigh(h, k):
        at = start_of(k)
        slot = h % 2
        top = mx_ref[slot]
        p = jnp.concatenate(
            [
                jnp.exp2(s_ref[slot, k, :, t * LANES : (t + 1) * LANES] * SCALE - top).astype(jnp.bfloat16)
                for t in range(KB // LANES)
            ],
            axis=1,
        )
        acc_ref[...] += jnp.dot(p, vx_ref[pl.ds(at, KB), :], preferred_element_type=jnp.float32)

    for phase in range(heads + 1):
        if phase < heads:
            mx_ref[phase % 2] = jnp.full((rows, LANES), NEG, jnp.float32)
        if phase > 0:
            acc_ref[...] = jnp.zeros_like(acc_ref)

        def body(k, _, phase=phase):
            if phase == heads:
                weigh(phase - 1, k)
                return 0
            at = first + k * KB
            interior = (at >= lo_max) & (at + KB <= hi_min)

            def run(masked):
                score(phase, k, masked)
                if phase > 0:
                    weigh(phase - 1, k)

            pl.when(interior)(lambda: run(False))
            pl.when(jnp.logical_not(interior))(lambda: run(True))
            return 0

        lax.fori_loop(0, blocks, body, 0)
        if phase < heads:
            top = jnp.max(mx_ref[phase % 2], axis=1, keepdims=True) * SCALE
            mx_ref[phase % 2] = jnp.broadcast_to(top, (rows, LANES))
        if phase > 0:
            h = phase - 1
            o_ref[:, h * HD : (h + 1) * HD] = (acc_ref[:, 0:HD] / acc_ref[:, HD : 2 * HD]).astype(jnp.bfloat16)


def attend(queries, kv, doc_ids, visible_end):
    rows, width = queries.shape
    seq = kv.shape[1]
    vmem = pl.BlockSpec(memory_space=pltpu.VMEM)
    return pl.pallas_call(
        attend_kernel,
        out_shape=jax.ShapeDtypeStruct((rows, width), jnp.bfloat16),
        in_specs=[vmem] * 4,
        out_specs=vmem,
        scratch_shapes=[
            pltpu.VMEM((2, seq // KB, rows, KB), jnp.float32),
            pltpu.VMEM((seq, 2 * HD), jnp.bfloat16),
            pltpu.VMEM((rows, 2 * HD), jnp.float32),
            pltpu.VMEM((2, rows, LANES), jnp.float32),
            pltpu.VMEM((rows, LANES), jnp.int32),
            pltpu.VMEM((rows, LANES), jnp.int32),
        ],
        compiler_params=pltpu.CompilerParams(vmem_limit_bytes=56 * 2**20),
        name="attend",
    )(queries, kv, doc_ids.reshape(-1, LANES), visible_end.reshape(1, rows))


def on_device(queries, keys, values, doc_ids, visible_end):
    kv = gather(keys, values, lax.axis_size("pb"))
    return attend(queries, kv, doc_ids, visible_end)


def solution(mesh):
    placed = (P("pb", None), P(("pb", "ka"), None), P(("pb", "ka"), None), P(), P("pb"))
    return jax.shard_map(
        on_device, mesh=mesh, in_specs=placed, out_specs=P("pb", None), check_vma=False
    )
```

```python
import functools

import jax
import jax.numpy as jnp
from jax import lax
from jax.experimental import pallas as pl
from jax.experimental.pallas import tpu as pltpu
from jax.sharding import PartitionSpec as P

HD = 128
NDOCS = 4
KB = 512
LANES = 128
NEG = -1e30
SCALE = 1.4426950408889634 / HD**0.5
MESH = pl.DeviceIdType.MESH


def gather_kernel(zs, k_ref, v_ref, out, col_s, col_r, x_s, x_r, y_s, y_r, fx_s, fx_r, fy_s, fy_r, c_s, c_r, own_s):
    p = lax.axis_index("pb")
    a = lax.axis_index("ka")
    n = k_ref.shape[0]
    z = p // 4
    r = p % 4
    y = r // 2
    c = r % 2
    row_y = z * 4 + (1 - y) * 2 + c
    core_p = z * 4 + y * 2 + (1 - c)
    x_peer = (p, 1 - a)
    y_peer = (row_y, a)
    core_peer = (core_p, a)

    def rows(src_z, ry, cc, aa):
        base = ((src_z * 4 + ry * 2 + cc) * 2 + aa) * n
        return pl.ds(pl.multiple_of(base, n), n)

    mine = rows(z, y, c, a)
    own = [
        pltpu.make_async_copy(src, out.at[kv, mine, :], own_s.at[kv])
        for kv, src in enumerate((k_ref, v_ref))
    ]
    for cp in own:
        cp.start()

    barrier = pltpu.get_barrier_semaphore()
    for peer in (x_peer, y_peer, core_peer):
        pl.semaphore_signal(barrier, inc=1, device_id=peer, device_id_type=MESH)
    for d in range(1, zs):
        pl.semaphore_signal(
            barrier, inc=1, device_id=(((z + d) % zs) * 4 + r, a), device_id_type=MESH
        )
    pl.semaphore_wait(barrier, 3 + zs - 1)
    for cp in own:
        cp.wait()

    def copy(view, ss, rs, peer):
        return pltpu.make_async_remote_copy(
            src_ref=view, dst_ref=view, send_sem=ss, recv_sem=rs, device_id=peer, device_id_type=MESH
        )

    def both(src_z, ry, cc, aa):
        return out.at[:, rows(src_z, ry, cc, aa), :]

    def one(kv, src_z, ry, cc, aa):
        return out.at[kv, rows(src_z, ry, cc, aa), :]

    order = []
    for step in range(1, zs // 2 + 1):
        for d in (step, zs - step):
            if 0 < d < zs and d not in order:
                order.append(d)
    sends = []

    def go(cp):
        cp.start()
        sends.append(cp)

    for d in order:
        go(copy(both(z, y, c, a), col_s.at[d], col_r.at[d], (((z + d) % zs) * 4 + r, a)))

    def spread(d):
        j = (z - d + zs) % zs
        go(copy(both(j, y, c, a), x_s.at[d], x_r.at[d], x_peer))
        go(copy(both(j, y, c, a), y_s.at[d], y_r.at[d], y_peer))
        go(copy(both(j, y, c, a), c_s.at[0, d], c_r.at[0, d], core_peer))

    def relay(d):
        j = (z - d + zs) % zs
        copy(both(j, y, c, 1 - a), x_s.at[d], x_r.at[d], x_peer).wait_recv()
        go(copy(one(0, j, y, c, 1 - a), fy_s.at[d], fy_r.at[d], y_peer))
        go(copy(both(j, y, c, 1 - a), c_s.at[1, d], c_r.at[1, d], core_peer))
        copy(both(j, 1 - y, c, a), y_s.at[d], y_r.at[d], y_peer).wait_recv()
        go(copy(one(1, j, 1 - y, c, a), fx_s.at[d], fx_r.at[d], x_peer))
        go(copy(both(j, 1 - y, c, a), c_s.at[2, d], c_r.at[2, d], core_peer))

    def last(d):
        j = (z - d + zs) % zs
        copy(one(0, j, 1 - y, c, 1 - a), fy_s.at[d], fy_r.at[d], y_peer).wait_recv()
        go(copy(one(0, j, 1 - y, c, 1 - a), c_s.at[3, d], c_r.at[3, d], core_peer))
        copy(one(1, j, 1 - y, c, 1 - a), fx_s.at[d], fx_r.at[d], x_peer).wait_recv()
        go(copy(one(1, j, 1 - y, c, 1 - a), c_s.at[4, d], c_r.at[4, d], core_peer))

    seq = [0] + order
    for i in range(zs + 2):
        if i < zs:
            d = seq[i]
            if d > 0:
                j = (z - d + zs) % zs
                copy(both(j, y, c, a), col_s.at[d], col_r.at[d], x_peer).wait_recv()
            spread(d)
        if 1 <= i < zs + 1:
            relay(seq[i - 1])
        if i >= 2:
            last(seq[i - 2])
    for d in seq:
        j = (z - d + zs) % zs
        copy(both(j, y, 1 - c, a), c_s.at[0, d], c_r.at[0, d], core_peer).wait_recv()
        copy(both(j, y, 1 - c, 1 - a), c_s.at[1, d], c_r.at[1, d], core_peer).wait_recv()
        copy(both(j, 1 - y, 1 - c, a), c_s.at[2, d], c_r.at[2, d], core_peer).wait_recv()
        copy(one(0, j, 1 - y, 1 - c, 1 - a), c_s.at[3, d], c_r.at[3, d], core_peer).wait_recv()
        copy(one(1, j, 1 - y, 1 - c, 1 - a), c_s.at[4, d], c_r.at[4, d], core_peer).wait_recv()
    for cp in sends:
        cp.wait_send()


def gather(keys, values, shards):
    zs = shards // 4
    n = keys.shape[0]
    dma = pltpu.SemaphoreType.DMA
    return pl.pallas_call(
        functools.partial(gather_kernel, zs),
        out_shape=jax.ShapeDtypeStruct((2, n * shards * 2, HD), jnp.bfloat16),
        in_specs=[pl.BlockSpec(memory_space=pltpu.HBM)] * 2,
        out_specs=pl.BlockSpec(memory_space=pltpu.VMEM),
        scratch_shapes=[dma((zs,))] * 10 + [dma((5, zs))] * 2 + [dma((2,))],
        compiler_params=pltpu.CompilerParams(
            collective_id=0, has_side_effects=True, vmem_limit_bytes=12 * 2**20
        ),
        name="gather_kv",
    )(keys, values)


def attend_kernel(hp, kb, q_ref, kv_ref, doc_ref, end_ref, o_ref, qs_ref, s_ref, kt_ref, vx_ref, acc_ref, mx_ref, lo_ref, hi_ref):
    rows = q_ref.shape[0]
    heads = q_ref.shape[1] // HD
    groups = heads // hp
    seq = kv_ref.shape[1]
    tall = hp * rows
    pos0 = lax.axis_index("pb") * rows
    docs = doc_ref[...]
    starts = [jnp.sum((docs < d).astype(jnp.int32)) for d in range(1, NDOCS)]
    pos = pos0 + lax.broadcasted_iota(jnp.int32, (1, rows), 1)
    lo = jnp.zeros((1, rows), jnp.int32)
    hi = jnp.minimum(end_ref[...], seq)
    for s in starts:
        lo = jnp.maximum(lo, jnp.where(pos >= s, s, 0))
        hi = jnp.minimum(hi, jnp.where(pos < s, s, seq))
    for t in range(rows // LANES):
        cut = slice(t * LANES, (t + 1) * LANES)
        lo_t = jnp.transpose(jnp.broadcast_to(lo[:, cut], (LANES, LANES)))
        hi_t = jnp.transpose(jnp.broadcast_to(hi[:, cut], (LANES, LANES)))
        for g in range(hp):
            lo_ref[pl.ds(g * rows + t * LANES, LANES), :] = lo_t
            hi_ref[pl.ds(g * rows + t * LANES, LANES), :] = hi_t
    for h in range(heads):
        qs_ref[h // hp, pl.ds((h % hp) * rows, rows), :] = q_ref[:, h * HD : (h + 1) * HD]
    lo_min = jnp.min(lo)
    lo_max = jnp.max(lo)
    hi_min = jnp.min(hi)
    hi_max = jnp.max(hi)
    first = (lo_min // LANES) * LANES
    blocks = (hi_max - first + kb - 1) // kb
    first = jnp.minimum(first, seq - blocks * kb)

    def start_of(k):
        return pl.multiple_of(first + k * kb, LANES)

    lanes = lax.broadcasted_iota(jnp.int32, (tall, LANES), 1)

    def fill(k, _):
        at = start_of(k)
        kt_ref[k] = jnp.transpose(kv_ref[0, pl.ds(at, kb), :])
        vx_ref[k, :, 0:HD] = kv_ref[1, pl.ds(at, kb), :]
        vx_ref[k, :, HD : 2 * HD] = jnp.ones((kb, HD), jnp.bfloat16)
        return 0

    lax.fori_loop(0, blocks, fill, 0)

    def score(g, k, masked):
        slot = g % 2
        s = jnp.dot(qs_ref[g], kt_ref[k], preferred_element_type=jnp.float32)
        top = mx_ref[slot]
        if masked:
            at = first + k * kb
            lo_at = lo_ref[...] - at
            hi_at = hi_ref[...] - at
        for t in range(kb // LANES):
            part = s[:, t * LANES : (t + 1) * LANES]
            if masked:
                where = lanes + t * LANES
                part = jnp.where((where >= lo_at) & (where < hi_at), part, NEG)
            s_ref[slot, k, :, t * LANES : (t + 1) * LANES] = part
            top = jnp.maximum(top, part)
        mx_ref[slot] = top

    def weigh(g, k):
        slot = g % 2
        top = mx_ref[slot]
        p = jnp.concatenate(
            [
                jnp.exp2(s_ref[slot, k, :, t * LANES : (t + 1) * LANES] * SCALE - top).astype(jnp.bfloat16)
                for t in range(kb // LANES)
            ],
            axis=1,
        )
        acc_ref[...] += jnp.dot(p, vx_ref[k], preferred_element_type=jnp.float32)

    for phase in range(groups + 1):
        if phase < groups:
            mx_ref[phase % 2] = jnp.full((tall, LANES), NEG, jnp.float32)
        if phase > 0:
            acc_ref[...] = jnp.zeros_like(acc_ref)

        def body(k, _, phase=phase):
            if phase == groups:
                weigh(phase - 1, k)
                return 0
            at = first + k * kb
            interior = (at >= lo_max) & (at + kb <= hi_min)

            def run(masked):
                score(phase, k, masked)
                if phase > 0:
                    weigh(phase - 1, k)

            pl.when(interior)(lambda: run(False))
            pl.when(jnp.logical_not(interior))(lambda: run(True))
            return 0

        lax.fori_loop(0, blocks, body, 0)
        if phase < groups:
            top = jnp.max(mx_ref[phase % 2], axis=1, keepdims=True) * SCALE
            mx_ref[phase % 2] = jnp.broadcast_to(top, (tall, LANES))
        if phase > 0:
            for g in range(hp):
                h = (phase - 1) * hp + g
                cut = pl.ds(g * rows, rows)
                o_ref[:, h * HD : (h + 1) * HD] = (
                    acc_ref[cut, 0:HD] / acc_ref[cut, HD : 2 * HD]
                ).astype(jnp.bfloat16)


def attend(queries, kv, doc_ids, visible_end, hp=0, kb=KB):
    rows, width = queries.shape
    heads = width // HD
    seq = kv.shape[1]
    if hp == 0:
        hp = 4 if seq <= 4096 else 1
    tall = hp * rows
    vmem = pl.BlockSpec(memory_space=pltpu.VMEM)
    need = 2 * seq * tall * 4 + seq * HD * 16 + 8 * 2**20
    return pl.pallas_call(
        functools.partial(attend_kernel, hp, kb),
        out_shape=jax.ShapeDtypeStruct((rows, width), jnp.bfloat16),
        in_specs=[vmem] * 4,
        out_specs=vmem,
        scratch_shapes=[
            pltpu.VMEM((heads // hp, tall, HD), jnp.bfloat16),
            pltpu.VMEM((2, seq // kb, tall, kb), jnp.float32),
            pltpu.VMEM((seq // kb, HD, kb), jnp.bfloat16),
            pltpu.VMEM((seq // kb, kb, 2 * HD), jnp.bfloat16),
            pltpu.VMEM((tall, 2 * HD), jnp.float32),
            pltpu.VMEM((2, tall, LANES), jnp.float32),
            pltpu.VMEM((tall, LANES), jnp.int32),
            pltpu.VMEM((tall, LANES), jnp.int32),
        ],
        compiler_params=pltpu.CompilerParams(vmem_limit_bytes=min(need, 58 * 2**20)),
        name="attend",
    )(queries, kv, doc_ids.reshape(-1, LANES), visible_end.reshape(1, rows))


def on_device(queries, keys, values, doc_ids, visible_end):
    kv = gather(keys, values, lax.axis_size("pb"))
    return attend(queries, kv, doc_ids, visible_end)


def solution(mesh):
    placed = (P("pb", None), P(("pb", "ka"), None), P(("pb", "ka"), None), P(), P("pb"))
    return jax.shard_map(
        on_device, mesh=mesh, in_specs=placed, out_specs=P("pb", None), check_vma=False
    )
```

```python
import functools

import jax
import jax.numpy as jnp
from jax import lax
from jax.experimental import pallas as pl
from jax.experimental.pallas import tpu as pltpu
from jax.sharding import PartitionSpec as P

HD = 128
NDOCS = 4
KB = 256
LANES = 128
NEG = -1e30
SCALE = 1.4426950408889634 / HD**0.5
MESH = pl.DeviceIdType.MESH


def gather_kernel(zs, k_ref, v_ref, out, col_s, col_r, x_s, x_r, y_s, y_r, fx_s, fx_r, fy_s, fy_r, c_s, c_r, own_s):
    p = lax.axis_index("pb")
    a = lax.axis_index("ka")
    n = k_ref.shape[0]
    z = p // 4
    r = p % 4
    y = r // 2
    c = r % 2
    row_y = z * 4 + (1 - y) * 2 + c
    core_p = z * 4 + y * 2 + (1 - c)
    x_peer = (p, 1 - a)
    y_peer = (row_y, a)
    core_peer = (core_p, a)

    def rows(src_z, ry, cc, aa):
        base = ((src_z * 4 + ry * 2 + cc) * 2 + aa) * n
        return pl.ds(pl.multiple_of(base, n), n)

    mine = rows(z, y, c, a)
    own = [
        pltpu.make_async_copy(src, out.at[kv, mine, :], own_s.at[kv])
        for kv, src in enumerate((k_ref, v_ref))
    ]
    for cp in own:
        cp.start()

    barrier = pltpu.get_barrier_semaphore()
    for peer in (x_peer, y_peer, core_peer, (row_y, 1 - a)):
        pl.semaphore_signal(barrier, inc=1, device_id=peer, device_id_type=MESH)
    for d in range(1, zs):
        pl.semaphore_signal(
            barrier, inc=1, device_id=(((z + d) % zs) * 4 + r, a), device_id_type=MESH
        )
    pl.semaphore_wait(barrier, 4 + zs - 1)
    for cp in own:
        cp.wait()

    def copy(view, ss, rs, peer):
        return pltpu.make_async_remote_copy(
            src_ref=view, dst_ref=view, send_sem=ss, recv_sem=rs, device_id=peer, device_id_type=MESH
        )

    def both(src_z, ry, cc, aa):
        return out.at[:, rows(src_z, ry, cc, aa), :]

    def one(kv, src_z, ry, cc, aa):
        return out.at[kv, rows(src_z, ry, cc, aa), :]

    order = []
    for step in range(1, zs // 2 + 1):
        for d in (step, zs - step):
            if 0 < d < zs and d not in order:
                order.append(d)
    sends = []

    def go(cp):
        cp.start()
        sends.append(cp)

    for d in order:
        go(copy(both(z, y, c, a), col_s.at[d], col_r.at[d], (((z + d) % zs) * 4 + r, a)))

    def spread(d):
        j = (z - d + zs) % zs
        go(copy(both(j, y, c, a), x_s.at[d], x_r.at[d], x_peer))
        go(copy(both(j, y, c, a), y_s.at[d], y_r.at[d], y_peer))
        go(copy(both(j, y, c, a), fy_s.at[d], fy_r.at[d], (row_y, 1 - a)))
        go(copy(both(j, y, c, a), c_s.at[0, d], c_r.at[0, d], core_peer))

    def relay(d):
        j = (z - d + zs) % zs
        copy(both(j, y, c, 1 - a), x_s.at[d], x_r.at[d], x_peer).wait_recv()
        go(copy(both(j, y, c, 1 - a), c_s.at[1, d], c_r.at[1, d], core_peer))
        copy(both(j, 1 - y, c, a), y_s.at[d], y_r.at[d], y_peer).wait_recv()
        go(copy(both(j, 1 - y, c, a), c_s.at[2, d], c_r.at[2, d], core_peer))
        copy(both(j, 1 - y, c, 1 - a), fy_s.at[d], fy_r.at[d], y_peer).wait_recv()
        go(copy(both(j, 1 - y, c, 1 - a), c_s.at[3, d], c_r.at[3, d], core_peer))

    def last(d):
        pass

    seq = [0] + order
    for d in seq:
        if d > 0:
            j = (z - d + zs) % zs
            copy(both(j, y, c, a), col_s.at[d], col_r.at[d], x_peer).wait_recv()
        spread(d)
    for d in seq:
        relay(d)
    for d in seq:
        last(d)
    for d in seq:
        j = (z - d + zs) % zs
        copy(both(j, y, 1 - c, a), c_s.at[0, d], c_r.at[0, d], core_peer).wait_recv()
        copy(both(j, y, 1 - c, 1 - a), c_s.at[1, d], c_r.at[1, d], core_peer).wait_recv()
        copy(both(j, 1 - y, 1 - c, a), c_s.at[2, d], c_r.at[2, d], core_peer).wait_recv()
        copy(both(j, 1 - y, 1 - c, 1 - a), c_s.at[3, d], c_r.at[3, d], core_peer).wait_recv()
    for cp in sends:
        cp.wait_send()


def gather(keys, values, shards):
    zs = shards // 4
    n = keys.shape[0]
    dma = pltpu.SemaphoreType.DMA
    return pl.pallas_call(
        functools.partial(gather_kernel, zs),
        out_shape=jax.ShapeDtypeStruct((2, n * shards * 2, HD), jnp.bfloat16),
        in_specs=[pl.BlockSpec(memory_space=pltpu.HBM)] * 2,
        out_specs=pl.BlockSpec(memory_space=pltpu.VMEM),
        scratch_shapes=[dma((zs,))] * 10 + [dma((5, zs))] * 2 + [dma((2,))],
        compiler_params=pltpu.CompilerParams(
            collective_id=0, has_side_effects=True, vmem_limit_bytes=12 * 2**20
        ),
        name="gather_kv",
    )(keys, values)


def attend_kernel(hp, kb, many, q_ref, kv_ref, doc_ref, end_ref, o_ref, qs_ref, s_ref, kt_ref, vx_ref, acc_ref, mx_ref, lo_ref, hi_ref):
    rows = q_ref.shape[0]
    heads = q_ref.shape[1] // HD
    groups = heads // hp
    seq = kv_ref.shape[1]
    tall = hp * rows
    pos0 = lax.axis_index("pb") * rows
    docs = doc_ref[...]
    starts = [jnp.sum((docs < d).astype(jnp.int32)) for d in range(1, NDOCS)]
    pos = pos0 + lax.broadcasted_iota(jnp.int32, (1, rows), 1)
    lo = jnp.zeros((1, rows), jnp.int32)
    hi = jnp.minimum(end_ref[...], seq)
    for s in starts:
        lo = jnp.maximum(lo, jnp.where(pos >= s, s, 0))
        hi = jnp.minimum(hi, jnp.where(pos < s, s, seq))
    for t in range(rows // LANES):
        cut = slice(t * LANES, (t + 1) * LANES)
        lo_t = jnp.transpose(jnp.broadcast_to(lo[:, cut], (LANES, LANES)))
        hi_t = jnp.transpose(jnp.broadcast_to(hi[:, cut], (LANES, LANES)))
        for g in range(hp):
            lo_ref[pl.ds(g * rows + t * LANES, LANES), :] = lo_t
            hi_ref[pl.ds(g * rows + t * LANES, LANES), :] = hi_t
    for h in range(heads):
        qs_ref[h // hp, pl.ds((h % hp) * rows, rows), :] = q_ref[:, h * HD : (h + 1) * HD]
    lo_min = jnp.min(lo)
    lo_max = jnp.max(lo)
    hi_min = jnp.min(hi)
    hi_max = jnp.max(hi)
    first = (lo_min // LANES) * LANES
    blocks = (hi_max - first + kb - 1) // kb
    first = jnp.minimum(first, seq - blocks * kb)

    def start_of(k):
        return pl.multiple_of(first + k * kb, LANES)

    lanes = lax.broadcasted_iota(jnp.int32, (tall, LANES), 1)

    def fill(k, _):
        at = start_of(k)
        kt_ref[k] = jnp.transpose(kv_ref[0, pl.ds(at, kb), :])
        here = pl.ds(pl.multiple_of(k * kb, kb), kb)
        vx_ref[here, 0:HD] = kv_ref[1, pl.ds(at, kb), :]
        vx_ref[here, HD : 2 * HD] = jnp.ones((kb, HD), jnp.bfloat16)
        return 0

    lax.fori_loop(0, blocks, fill, 0)

    def score(g, k0, count, masked):
        slot = g % 2
        top = mx_ref[slot]
        for k in [k0 + i for i in range(count)]:
            s = jnp.dot(qs_ref[g], kt_ref[k], preferred_element_type=jnp.float32)
            if masked:
                at = first + k * kb
                lo_at = lo_ref[...] - at
                hi_at = hi_ref[...] - at
            for t in range(kb // LANES):
                part = s[:, t * LANES : (t + 1) * LANES]
                if masked:
                    where = lanes + t * LANES
                    part = jnp.where((where >= lo_at) & (where < hi_at), part, NEG)
                s_ref[slot, k, :, t * LANES : (t + 1) * LANES] = part
                top = jnp.maximum(top, part)
        mx_ref[slot] = top

    def weigh(g, k0, count):
        slot = g % 2
        top = mx_ref[slot]
        p = jnp.concatenate(
            [
                jnp.exp2(s_ref[slot, k0 + i, :, t * LANES : (t + 1) * LANES] * SCALE - top).astype(jnp.bfloat16)
                for i in range(count)
                for t in range(kb // LANES)
            ],
            axis=1,
        )
        here = pl.ds(pl.multiple_of(k0 * kb, kb), count * kb)
        acc_ref[...] += jnp.dot(p, vx_ref[here, :], preferred_element_type=jnp.float32)

    for phase in range(groups + 1):
        if phase < groups:
            mx_ref[phase % 2] = jnp.full((tall, LANES), NEG, jnp.float32)
        if phase > 0:
            acc_ref[...] = jnp.zeros_like(acc_ref)

        def visit(k, count, phase=phase):
            if phase == groups:
                weigh(phase - 1, k, count)
                return
            at = first + k * kb
            interior = (at >= lo_max) & (at + count * kb <= hi_min)

            def run(masked):
                score(phase, k, count, masked)
                if phase > 0:
                    weigh(phase - 1, k, count)

            pl.when(interior)(lambda: run(False))
            pl.when(jnp.logical_not(interior))(lambda: run(True))

        def wide(i, _, visit=visit):
            visit(i * many, many)
            return 0

        def single(k, _, visit=visit):
            visit(k, 1)
            return 0

        whole = blocks // many
        lax.fori_loop(0, whole, wide, 0)
        if many > 1:
            lax.fori_loop(whole * many, blocks, single, 0)
        if phase < groups:
            top = jnp.max(mx_ref[phase % 2], axis=1, keepdims=True) * SCALE
            mx_ref[phase % 2] = jnp.broadcast_to(top, (tall, LANES))
        if phase > 0:
            for g in range(hp):
                h = (phase - 1) * hp + g
                cut = pl.ds(g * rows, rows)
                o_ref[:, h * HD : (h + 1) * HD] = (
                    acc_ref[cut, 0:HD] / acc_ref[cut, HD : 2 * HD]
                ).astype(jnp.bfloat16)


def attend(queries, kv, doc_ids, visible_end, hp=0, kb=KB, many=4):
    rows, width = queries.shape
    heads = width // HD
    seq = kv.shape[1]
    if hp == 0:
        hp = 4 if seq <= 4096 else 1
    tall = hp * rows
    vmem = pl.BlockSpec(memory_space=pltpu.VMEM)
    need = 2 * seq * tall * 4 + seq * HD * 16 + 8 * 2**20
    return pl.pallas_call(
        functools.partial(attend_kernel, hp, kb, many),
        out_shape=jax.ShapeDtypeStruct((rows, width), jnp.bfloat16),
        in_specs=[vmem] * 4,
        out_specs=vmem,
        scratch_shapes=[
            pltpu.VMEM((heads // hp, tall, HD), jnp.bfloat16),
            pltpu.VMEM((2, seq // kb, tall, kb), jnp.float32),
            pltpu.VMEM((seq // kb, HD, kb), jnp.bfloat16),
            pltpu.VMEM((seq, 2 * HD), jnp.bfloat16),
            pltpu.VMEM((tall, 2 * HD), jnp.float32),
            pltpu.VMEM((2, tall, LANES), jnp.float32),
            pltpu.VMEM((tall, LANES), jnp.int32),
            pltpu.VMEM((tall, LANES), jnp.int32),
        ],
        compiler_params=pltpu.CompilerParams(vmem_limit_bytes=min(need, 58 * 2**20)),
        name="attend",
    )(queries, kv, doc_ids.reshape(-1, LANES), visible_end.reshape(1, rows))


def on_device(queries, keys, values, doc_ids, visible_end):
    kv = gather(keys, values, lax.axis_size("pb"))
    return attend(queries, kv, doc_ids, visible_end)


def solution(mesh):
    placed = (P("pb", None), P(("pb", "ka"), None), P(("pb", "ka"), None), P(), P("pb"))
    return jax.shard_map(
        on_device, mesh=mesh, in_specs=placed, out_specs=P("pb", None), check_vma=False
    )
```

```python
import functools

import jax
import jax.numpy as jnp
from jax import lax
from jax.experimental import pallas as pl
from jax.experimental.pallas import tpu as pltpu
from jax.sharding import PartitionSpec as P

HD = 128
NDOCS = 4
KB = 256
LANES = 128
NEG = -1e30
SCALE = 1.4426950408889634 / HD**0.5
MESH = pl.DeviceIdType.MESH


def gather_kernel(zs, k_ref, v_ref, out, col_s, col_r, x_s, x_r, y_s, y_r, fx_s, fx_r, fy_s, fy_r, c_s, c_r, own_s):
    p = lax.axis_index("pb")
    a = lax.axis_index("ka")
    n = k_ref.shape[0]
    z = p // 4
    r = p % 4
    y = r // 2
    c = r % 2
    row_y = z * 4 + (1 - y) * 2 + c
    core_p = z * 4 + y * 2 + (1 - c)
    x_peer = (p, 1 - a)
    y_peer = (row_y, a)
    core_peer = (core_p, a)

    def rows(src_z, ry, cc, aa):
        base = ((src_z * 4 + ry * 2 + cc) * 2 + aa) * n
        return pl.ds(pl.multiple_of(base, n), n)

    mine = rows(z, y, c, a)
    own = [
        pltpu.make_async_copy(src, out.at[kv, mine, :], own_s.at[kv])
        for kv, src in enumerate((k_ref, v_ref))
    ]
    for cp in own:
        cp.start()

    barrier = pltpu.get_barrier_semaphore()
    for peer in (x_peer, y_peer, core_peer, (row_y, 1 - a)):
        pl.semaphore_signal(barrier, inc=1, device_id=peer, device_id_type=MESH)
    for d in range(1, zs):
        pl.semaphore_signal(
            barrier, inc=1, device_id=(((z + d) % zs) * 4 + r, a), device_id_type=MESH
        )
    pl.semaphore_wait(barrier, 4 + zs - 1)
    for cp in own:
        cp.wait()

    def copy(view, ss, rs, peer):
        return pltpu.make_async_remote_copy(
            src_ref=view, dst_ref=view, send_sem=ss, recv_sem=rs, device_id=peer, device_id_type=MESH
        )

    def both(src_z, ry, cc, aa):
        return out.at[:, rows(src_z, ry, cc, aa), :]

    def one(kv, src_z, ry, cc, aa):
        return out.at[kv, rows(src_z, ry, cc, aa), :]

    order = []
    for step in range(1, zs // 2 + 1):
        for d in (step, zs - step):
            if 0 < d < zs and d not in order:
                order.append(d)
    sends = []

    def go(cp):
        cp.start()
        sends.append(cp)

    for d in order:
        go(copy(both(z, y, c, a), col_s.at[d], col_r.at[d], (((z + d) % zs) * 4 + r, a)))

    def spread(d):
        j = (z - d + zs) % zs
        go(copy(both(j, y, c, a), x_s.at[d], x_r.at[d], x_peer))
        go(copy(both(j, y, c, a), y_s.at[d], y_r.at[d], y_peer))
        go(copy(both(j, y, c, a), fy_s.at[d], fy_r.at[d], (row_y, 1 - a)))
        go(copy(both(j, y, c, a), c_s.at[0, d], c_r.at[0, d], core_peer))

    def relay(d):
        j = (z - d + zs) % zs
        copy(both(j, y, c, 1 - a), x_s.at[d], x_r.at[d], x_peer).wait_recv()
        go(copy(both(j, y, c, 1 - a), c_s.at[1, d], c_r.at[1, d], core_peer))
        copy(both(j, 1 - y, c, a), y_s.at[d], y_r.at[d], y_peer).wait_recv()
        go(copy(both(j, 1 - y, c, a), c_s.at[2, d], c_r.at[2, d], core_peer))
        copy(both(j, 1 - y, c, 1 - a), fy_s.at[d], fy_r.at[d], y_peer).wait_recv()
        go(copy(both(j, 1 - y, c, 1 - a), c_s.at[3, d], c_r.at[3, d], core_peer))

    def last(d):
        pass

    seq = [0] + order
    for d in seq:
        if d > 0:
            j = (z - d + zs) % zs
            copy(both(j, y, c, a), col_s.at[d], col_r.at[d], x_peer).wait_recv()
        spread(d)
    for d in seq:
        relay(d)
    for d in seq:
        last(d)
    for d in seq:
        j = (z - d + zs) % zs
        copy(both(j, y, 1 - c, a), c_s.at[0, d], c_r.at[0, d], core_peer).wait_recv()
        copy(both(j, y, 1 - c, 1 - a), c_s.at[1, d], c_r.at[1, d], core_peer).wait_recv()
        copy(both(j, 1 - y, 1 - c, a), c_s.at[2, d], c_r.at[2, d], core_peer).wait_recv()
        copy(both(j, 1 - y, 1 - c, 1 - a), c_s.at[3, d], c_r.at[3, d], core_peer).wait_recv()
    for cp in sends:
        cp.wait_send()


def gather(keys, values, shards):
    zs = shards // 4
    n = keys.shape[0]
    dma = pltpu.SemaphoreType.DMA
    return pl.pallas_call(
        functools.partial(gather_kernel, zs),
        out_shape=jax.ShapeDtypeStruct((2, n * shards * 2, HD), jnp.bfloat16),
        in_specs=[pl.BlockSpec(memory_space=pltpu.HBM)] * 2,
        out_specs=pl.BlockSpec(memory_space=pltpu.VMEM),
        scratch_shapes=[dma((zs,))] * 10 + [dma((5, zs))] * 2 + [dma((2,))],
        compiler_params=pltpu.CompilerParams(
            collective_id=0, has_side_effects=True, vmem_limit_bytes=12 * 2**20
        ),
        name="gather_kv",
    )(keys, values)


def attend_kernel(hp, kb, many, q_ref, kv_ref, doc_ref, end_ref, o_ref, qs_ref, s_ref, kt_ref, vx_ref, acc_ref, mx_ref, lo_ref, hi_ref):
    rows = q_ref.shape[0]
    heads = q_ref.shape[1] // HD
    groups = heads // hp
    seq = kv_ref.shape[1]
    tall = hp * rows
    pos0 = lax.axis_index("pb") * rows
    docs = doc_ref[...]
    starts = [jnp.sum((docs < d).astype(jnp.int32)) for d in range(1, NDOCS)]
    pos = pos0 + lax.broadcasted_iota(jnp.int32, (1, rows), 1)
    lo = jnp.zeros((1, rows), jnp.int32)
    hi = jnp.minimum(end_ref[...], seq)
    for s in starts:
        lo = jnp.maximum(lo, jnp.where(pos >= s, s, 0))
        hi = jnp.minimum(hi, jnp.where(pos < s, s, seq))
    for t in range(rows // LANES):
        cut = slice(t * LANES, (t + 1) * LANES)
        lo_t = jnp.transpose(jnp.broadcast_to(lo[:, cut], (LANES, LANES)))
        hi_t = jnp.transpose(jnp.broadcast_to(hi[:, cut], (LANES, LANES)))
        for g in range(hp):
            lo_ref[pl.ds(g * rows + t * LANES, LANES), :] = lo_t
            hi_ref[pl.ds(g * rows + t * LANES, LANES), :] = hi_t
    for h in range(heads):
        qs_ref[h // hp, pl.ds((h % hp) * rows, rows), :] = q_ref[:, h * HD : (h + 1) * HD]
    lo_min = jnp.min(lo)
    lo_max = jnp.max(lo)
    hi_min = jnp.min(hi)
    hi_max = jnp.max(hi)
    first = (lo_min // LANES) * LANES
    blocks = (hi_max - first + kb - 1) // kb
    first = jnp.minimum(first, seq - blocks * kb)

    def start_of(k):
        return pl.multiple_of(first + k * kb, LANES)

    lanes = lax.broadcasted_iota(jnp.int32, (tall, LANES), 1)

    def fill(k, _):
        at = start_of(k)
        kt_ref[k] = jnp.transpose(kv_ref[0, pl.ds(at, kb), :])
        here = pl.ds(pl.multiple_of(k * kb, kb), kb)
        vx_ref[here, 0:HD] = kv_ref[1, pl.ds(at, kb), :]
        vx_ref[here, HD : 2 * HD] = jnp.ones((kb, HD), jnp.bfloat16)
        return 0

    lax.fori_loop(0, blocks, fill, 0)

    def score(g, k0, count, masked):
        slot = g % 2
        top = mx_ref[slot]
        for k in [k0 + i for i in range(count)]:
            s = jnp.dot(qs_ref[g], kt_ref[k], preferred_element_type=jnp.float32)
            if masked:
                at = first + k * kb
                lo_at = lo_ref[...] - at
                hi_at = hi_ref[...] - at
            for t in range(kb // LANES):
                part = s[:, t * LANES : (t + 1) * LANES]
                if masked:
                    where = lanes + t * LANES
                    part = jnp.where((where >= lo_at) & (where < hi_at), part, NEG)
                s_ref[slot, k, :, t * LANES : (t + 1) * LANES] = part
                top = jnp.maximum(top, part)
        mx_ref[slot] = top

    def weigh(g, k0, count):
        slot = g % 2
        top = mx_ref[slot]
        p = jnp.concatenate(
            [
                jnp.exp2(s_ref[slot, k0 + i, :, t * LANES : (t + 1) * LANES] * SCALE - top).astype(jnp.bfloat16)
                for i in range(count)
                for t in range(kb // LANES)
            ],
            axis=1,
        )
        here = pl.ds(pl.multiple_of(k0 * kb, kb), count * kb)
        acc_ref[...] += jnp.dot(p, vx_ref[here, :], preferred_element_type=jnp.float32)

    for phase in range(groups + 1):
        if phase < groups:
            mx_ref[phase % 2] = jnp.full((tall, LANES), NEG, jnp.float32)
        if phase > 0:
            acc_ref[...] = jnp.zeros_like(acc_ref)

        def visit(k, count, phase=phase):
            if phase == groups:
                weigh(phase - 1, k, count)
                return
            at = first + k * kb
            interior = (at >= lo_max) & (at + count * kb <= hi_min)

            def run(masked):
                score(phase, k, count, masked)
                if phase > 0:
                    weigh(phase - 1, k, count)

            pl.when(interior)(lambda: run(False))
            pl.when(jnp.logical_not(interior))(lambda: run(True))

        def wide(i, _, visit=visit):
            visit(i * many, many)
            return 0

        def single(k, _, visit=visit):
            visit(k, 1)
            return 0

        whole = blocks // many
        lax.fori_loop(0, whole, wide, 0)
        if many > 1:
            lax.fori_loop(whole * many, blocks, single, 0)
        if phase < groups:
            top = jnp.max(mx_ref[phase % 2], axis=1, keepdims=True) * SCALE
            mx_ref[phase % 2] = jnp.broadcast_to(top, (tall, LANES))
        if phase > 0:
            for g in range(hp):
                h = (phase - 1) * hp + g
                cut = pl.ds(g * rows, rows)
                o_ref[:, h * HD : (h + 1) * HD] = (
                    acc_ref[cut, 0:HD] / acc_ref[cut, HD : 2 * HD]
                ).astype(jnp.bfloat16)


def attend(queries, kv, doc_ids, visible_end, hp=0, kb=KB, many=4):
    rows, width = queries.shape
    heads = width // HD
    seq = kv.shape[1]
    if hp == 0:
        hp = 4 if seq <= 4096 else 1
    tall = hp * rows
    vmem = pl.BlockSpec(memory_space=pltpu.VMEM)
    need = 2 * seq * tall * 4 + seq * HD * 16 + 8 * 2**20
    return pl.pallas_call(
        functools.partial(attend_kernel, hp, kb, many),
        out_shape=jax.ShapeDtypeStruct((rows, width), jnp.bfloat16),
        in_specs=[vmem] * 4,
        out_specs=vmem,
        scratch_shapes=[
            pltpu.VMEM((heads // hp, tall, HD), jnp.bfloat16),
            pltpu.VMEM((2, seq // kb, tall, kb), jnp.float32),
            pltpu.VMEM((seq // kb, HD, kb), jnp.bfloat16),
            pltpu.VMEM((seq, 2 * HD), jnp.bfloat16),
            pltpu.VMEM((tall, 2 * HD), jnp.float32),
            pltpu.VMEM((2, tall, LANES), jnp.float32),
            pltpu.VMEM((tall, LANES), jnp.int32),
            pltpu.VMEM((tall, LANES), jnp.int32),
        ],
        compiler_params=pltpu.CompilerParams(vmem_limit_bytes=min(need, 58 * 2**20)),
        name="attend",
    )(queries, kv, doc_ids.reshape(-1, LANES), visible_end.reshape(1, rows))


def on_device(queries, keys, values, doc_ids, visible_end):
    keys = pltpu.with_memory_space_constraint(keys, pltpu.HBM)
    values = pltpu.with_memory_space_constraint(values, pltpu.HBM)
    kv = gather(keys, values, lax.axis_size("pb"))
    return attend(queries, kv, doc_ids, visible_end)


def solution(mesh):
    placed = (P("pb", None), P(("pb", "ka"), None), P(("pb", "ka"), None), P(), P("pb"))
    return jax.shard_map(
        on_device, mesh=mesh, in_specs=placed, out_specs=P("pb", None), check_vma=False
    )
```

```python
import functools

import jax
import jax.numpy as jnp
from jax import lax
from jax.experimental import pallas as pl
from jax.experimental.pallas import tpu as pltpu
from jax.sharding import PartitionSpec as P

HD = 128
NDOCS = 4
KB = 256
LANES = 128
NEG = -1e30
SCALE = 1.4426950408889634 / HD**0.5
MESH = pl.DeviceIdType.MESH


def gather_kernel(zs, k_ref, v_ref, out, col_s, col_r, x_s, x_r, y_s, y_r, fx_s, fx_r, fy_s, fy_r, c_s, c_r, own_s):
    p = lax.axis_index("pb")
    a = lax.axis_index("ka")
    n = k_ref.shape[0]
    z = p // 4
    r = p % 4
    y = r // 2
    c = r % 2
    row_y = z * 4 + (1 - y) * 2 + c
    core_p = z * 4 + y * 2 + (1 - c)
    x_peer = (p, 1 - a)
    y_peer = (row_y, a)
    core_peer = (core_p, a)

    def rows(src_z, ry, cc, aa):
        base = ((src_z * 4 + ry * 2 + cc) * 2 + aa) * n
        return pl.ds(pl.multiple_of(base, n), n)

    mine = rows(z, y, c, a)
    own = [
        pltpu.make_async_copy(src, out.at[kv, mine, :], own_s.at[kv])
        for kv, src in enumerate((k_ref, v_ref))
    ]
    for cp in own:
        cp.start()

    barrier = pltpu.get_barrier_semaphore()
    for peer in (x_peer, y_peer, core_peer, (row_y, 1 - a)):
        pl.semaphore_signal(barrier, inc=1, device_id=peer, device_id_type=MESH)
    for d in range(1, zs):
        pl.semaphore_signal(
            barrier, inc=1, device_id=(((z + d) % zs) * 4 + r, a), device_id_type=MESH
        )
    pl.semaphore_wait(barrier, 4 + zs - 1)
    for cp in own:
        cp.wait()

    def copy(view, ss, rs, peer):
        return pltpu.make_async_remote_copy(
            src_ref=view, dst_ref=view, send_sem=ss, recv_sem=rs, device_id=peer, device_id_type=MESH
        )

    def both(src_z, ry, cc, aa):
        return out.at[:, rows(src_z, ry, cc, aa), :]

    def one(kv, src_z, ry, cc, aa):
        return out.at[kv, rows(src_z, ry, cc, aa), :]

    order = []
    for step in range(1, zs // 2 + 1):
        for d in (step, zs - step):
            if 0 < d < zs and d not in order:
                order.append(d)
    sends = []

    def go(cp):
        cp.start()
        sends.append(cp)

    for d in order:
        go(copy(both(z, y, c, a), col_s.at[d], col_r.at[d], (((z + d) % zs) * 4 + r, a)))

    def spread(d):
        j = (z - d + zs) % zs
        go(copy(both(j, y, c, a), x_s.at[d], x_r.at[d], x_peer))
        go(copy(both(j, y, c, a), y_s.at[d], y_r.at[d], y_peer))
        go(copy(both(j, y, c, a), fy_s.at[d], fy_r.at[d], (row_y, 1 - a)))
        go(copy(both(j, y, c, a), c_s.at[0, d], c_r.at[0, d], core_peer))

    def relay(d):
        j = (z - d + zs) % zs
        copy(both(j, y, c, 1 - a), x_s.at[d], x_r.at[d], x_peer).wait_recv()
        go(copy(both(j, y, c, 1 - a), c_s.at[1, d], c_r.at[1, d], core_peer))
        copy(both(j, 1 - y, c, a), y_s.at[d], y_r.at[d], y_peer).wait_recv()
        go(copy(both(j, 1 - y, c, a), c_s.at[2, d], c_r.at[2, d], core_peer))
        copy(both(j, 1 - y, c, 1 - a), fy_s.at[d], fy_r.at[d], y_peer).wait_recv()
        go(copy(both(j, 1 - y, c, 1 - a), c_s.at[3, d], c_r.at[3, d], core_peer))

    def last(d):
        pass

    seq = [0] + order
    for d in seq:
        if d > 0:
            j = (z - d + zs) % zs
            copy(both(j, y, c, a), col_s.at[d], col_r.at[d], x_peer).wait_recv()
        spread(d)
    for d in seq:
        relay(d)
    for d in seq:
        last(d)
    for d in seq:
        j = (z - d + zs) % zs
        copy(both(j, y, 1 - c, a), c_s.at[0, d], c_r.at[0, d], core_peer).wait_recv()
        copy(both(j, y, 1 - c, 1 - a), c_s.at[1, d], c_r.at[1, d], core_peer).wait_recv()
        copy(both(j, 1 - y, 1 - c, a), c_s.at[2, d], c_r.at[2, d], core_peer).wait_recv()
        copy(both(j, 1 - y, 1 - c, 1 - a), c_s.at[3, d], c_r.at[3, d], core_peer).wait_recv()
    for cp in sends:
        cp.wait_send()


def gather(keys, values, shards):
    zs = shards // 4
    n = keys.shape[0]
    dma = pltpu.SemaphoreType.DMA
    return pl.pallas_call(
        functools.partial(gather_kernel, zs),
        out_shape=jax.ShapeDtypeStruct((2, n * shards * 2, HD), jnp.bfloat16),
        in_specs=[pl.BlockSpec(memory_space=pltpu.HBM)] * 2,
        out_specs=pl.BlockSpec(memory_space=pltpu.VMEM),
        scratch_shapes=[dma((zs,))] * 10 + [dma((5, zs))] * 2 + [dma((2,))],
        compiler_params=pltpu.CompilerParams(
            collective_id=0, has_side_effects=True, vmem_limit_bytes=12 * 2**20
        ),
        name="gather_kv",
    )(keys, values)


def attend_kernel(hp, kb, many, q_ref, kv_ref, doc_ref, end_ref, o_ref, qs_ref, s_ref, kt_ref, vx_ref, acc_ref, mx_ref, lo_ref, hi_ref):
    rows = q_ref.shape[0]
    heads = q_ref.shape[1] // HD
    groups = heads // hp
    seq = kv_ref.shape[1]
    tall = hp * rows
    pos0 = lax.axis_index("pb") * rows
    docs = doc_ref[...]
    starts = [jnp.sum((docs < d).astype(jnp.int32)) for d in range(1, NDOCS)]
    pos = pos0 + lax.broadcasted_iota(jnp.int32, (1, rows), 1)
    lo = jnp.zeros((1, rows), jnp.int32)
    hi = jnp.minimum(end_ref[...], seq)
    for s in starts:
        lo = jnp.maximum(lo, jnp.where(pos >= s, s, 0))
        hi = jnp.minimum(hi, jnp.where(pos < s, s, seq))
    for t in range(rows // LANES):
        cut = slice(t * LANES, (t + 1) * LANES)
        lo_t = jnp.transpose(jnp.broadcast_to(lo[:, cut], (LANES, LANES)))
        hi_t = jnp.transpose(jnp.broadcast_to(hi[:, cut], (LANES, LANES)))
        for g in range(hp):
            lo_ref[pl.ds(g * rows + t * LANES, LANES), :] = lo_t
            hi_ref[pl.ds(g * rows + t * LANES, LANES), :] = hi_t
    for h in range(heads):
        qs_ref[h // hp, pl.ds((h % hp) * rows, rows), :] = q_ref[:, h * HD : (h + 1) * HD]
    lo_min = jnp.min(lo)
    lo_max = jnp.max(lo)
    hi_min = jnp.min(hi)
    hi_max = jnp.max(hi)
    first = (lo_min // LANES) * LANES
    blocks = (hi_max - first + kb - 1) // kb
    first = jnp.minimum(first, seq - blocks * kb)

    def start_of(k):
        return pl.multiple_of(first + k * kb, LANES)

    lanes = lax.broadcasted_iota(jnp.int32, (tall, LANES), 1)

    def fill(k, _):
        at = start_of(k)
        kt_ref[k] = jnp.transpose(kv_ref[0, pl.ds(at, kb), :])
        here = pl.ds(pl.multiple_of(k * kb, kb), kb)
        vx_ref[here, 0:HD] = kv_ref[1, pl.ds(at, kb), :]
        vx_ref[here, HD : 2 * HD] = jnp.ones((kb, HD), jnp.bfloat16)
        return 0

    lax.fori_loop(0, blocks, fill, 0)

    def score(g, k0, count, low, high):
        slot = g % 2
        top = mx_ref[slot]
        for k in [k0 + i for i in range(count)]:
            s = jnp.dot(qs_ref[g], kt_ref[k], preferred_element_type=jnp.float32)
            at = first + k * kb
            if low:
                lo_at = lo_ref[...] - at
            if high:
                hi_at = hi_ref[...] - at
            for t in range(kb // LANES):
                part = s[:, t * LANES : (t + 1) * LANES]
                where = lanes + t * LANES
                if low:
                    part = jnp.where(where >= lo_at, part, NEG)
                if high:
                    part = jnp.where(where < hi_at, part, NEG)
                s_ref[slot, k, :, t * LANES : (t + 1) * LANES] = part
                top = jnp.maximum(top, part)
        mx_ref[slot] = top

    def weigh(g, k0, count):
        slot = g % 2
        top = mx_ref[slot]
        p = jnp.concatenate(
            [
                jnp.exp2(s_ref[slot, k0 + i, :, t * LANES : (t + 1) * LANES] * SCALE - top).astype(jnp.bfloat16)
                for i in range(count)
                for t in range(kb // LANES)
            ],
            axis=1,
        )
        here = pl.ds(pl.multiple_of(k0 * kb, kb), count * kb)
        acc_ref[...] += jnp.dot(p, vx_ref[here, :], preferred_element_type=jnp.float32)

    for phase in range(groups + 1):
        if phase < groups:
            mx_ref[phase % 2] = jnp.full((tall, LANES), NEG, jnp.float32)
        if phase > 0:
            acc_ref[...] = jnp.zeros_like(acc_ref)

        def visit(k, count, phase=phase):
            if phase == groups:
                weigh(phase - 1, k, count)
                return
            at = first + k * kb
            low = at < lo_max
            high = at + count * kb > hi_min

            def run(on_low, on_high):
                score(phase, k, count, on_low, on_high)
                if phase > 0:
                    weigh(phase - 1, k, count)

            no_low = jnp.logical_not(low)
            no_high = jnp.logical_not(high)
            pl.when(no_low & no_high)(lambda: run(False, False))
            pl.when(low & no_high)(lambda: run(True, False))
            pl.when(no_low & high)(lambda: run(False, True))
            pl.when(low & high)(lambda: run(True, True))

        def wide(i, _, visit=visit):
            visit(i * many, many)
            return 0

        def single(k, _, visit=visit):
            visit(k, 1)
            return 0

        whole = blocks // many
        lax.fori_loop(0, whole, wide, 0)
        if many > 1:
            lax.fori_loop(whole * many, blocks, single, 0)
        if phase < groups:
            top = jnp.max(mx_ref[phase % 2], axis=1, keepdims=True) * SCALE
            mx_ref[phase % 2] = jnp.broadcast_to(top, (tall, LANES))
        if phase > 0:
            for g in range(hp):
                h = (phase - 1) * hp + g
                cut = pl.ds(g * rows, rows)
                o_ref[:, h * HD : (h + 1) * HD] = (
                    acc_ref[cut, 0:HD] / acc_ref[cut, HD : 2 * HD]
                ).astype(jnp.bfloat16)


def attend(queries, kv, doc_ids, visible_end, hp=0, kb=KB, many=4):
    rows, width = queries.shape
    heads = width // HD
    seq = kv.shape[1]
    if hp == 0:
        hp = 4 if seq <= 4096 else 1
    tall = hp * rows
    vmem = pl.BlockSpec(memory_space=pltpu.VMEM)
    need = 2 * seq * tall * 4 + seq * HD * 16 + 8 * 2**20
    return pl.pallas_call(
        functools.partial(attend_kernel, hp, kb, many),
        out_shape=jax.ShapeDtypeStruct((rows, width), jnp.bfloat16),
        in_specs=[vmem] * 4,
        out_specs=vmem,
        scratch_shapes=[
            pltpu.VMEM((heads // hp, tall, HD), jnp.bfloat16),
            pltpu.VMEM((2, seq // kb, tall, kb), jnp.float32),
            pltpu.VMEM((seq // kb, HD, kb), jnp.bfloat16),
            pltpu.VMEM((seq, 2 * HD), jnp.bfloat16),
            pltpu.VMEM((tall, 2 * HD), jnp.float32),
            pltpu.VMEM((2, tall, LANES), jnp.float32),
            pltpu.VMEM((tall, LANES), jnp.int32),
            pltpu.VMEM((tall, LANES), jnp.int32),
        ],
        compiler_params=pltpu.CompilerParams(vmem_limit_bytes=min(need, 58 * 2**20)),
        name="attend",
    )(queries, kv, doc_ids.reshape(-1, LANES), visible_end.reshape(1, rows))


def on_device(queries, keys, values, doc_ids, visible_end):
    keys = pltpu.with_memory_space_constraint(keys, pltpu.HBM)
    values = pltpu.with_memory_space_constraint(values, pltpu.HBM)
    kv = gather(keys, values, lax.axis_size("pb"))
    return attend(queries, kv, doc_ids, visible_end)


def solution(mesh):
    placed = (P("pb", None), P(("pb", "ka"), None), P(("pb", "ka"), None), P(), P("pb"))
    return jax.shard_map(
        on_device, mesh=mesh, in_specs=placed, out_specs=P("pb", None), check_vma=False
    )
```
